32 devices in a mesh: frow: 4 (over y, x), fcol: 8 (over z, core).
Axes of the slice: x: 2, y: 2, z: 4, core: 2. Of those that a mesh axis runs over, the one named last changes fastest.
Arguments:
- strips: bfloat16 [2, 256, 32768], P(None, 'frow', 'fcol'), may hold values from -6 to 6
- row_window: float32 [4096], replicated, may hold values from 0.5 to 2
- col_window: float32 [4096], replicated, may hold values from 0.5 to 2
- sub_rows: int32 [4], replicated, may hold values from 0 to 65535
- sub_cols: int32 [4], replicated, may hold values from 0 to 65535
- facet_offsets: int32 [4, 8, 2], replicated, may hold values from 0 to 65472, as said below
- owner_map: int32 [32], replicated, may hold values from 0 to 31, each once
- screens: float32 [2, 32, 512, 256], P(None, 'fcol', 'frow'), may hold values from -1.5 to 1.5
Outputs:
- subgrids: float32 [2, 32, 512, 256], P(None, 'fcol', 'frow')
The draws below stay inside these ranges and needn't reach their ends.
Inputs may be any that keep to these rules, and one draw needn't show every extreme that they name: `facet_offsets`: entry [a, b, 0] is a multiple of 64 whose 64 rows stay within one facet of 4096 rows; entry [a, b, 1] is a multiple of 4096.
All inputs are finite; a program needn't handle non-finite values.
Results may differ from the reference program's by a relative error of at most 0.0066.
Values may be sent and summed in bfloat16 or wider, within the bound.
A program may use at most 128 MiB of HBM per device.

```python
import math
import jax
import jax.numpy as jnp
from jax import lax

N = 65536
F = 4096
R = 64
M = 128
S = 512
SG_R = 4
SG_C = 4
PIECES = 32
N_FROW = 4
N_FCOL = 8


def draw_facet_offsets(key, part):
    key_rows = jax.random.fold_in(key, 11)
    key_strip = jax.random.fold_in(key, 12)
    key_cols = jax.random.fold_in(key, 13)
    facet_row = jax.random.randint(key_rows, (N_FROW, N_FCOL), 0, N // F, dtype=jnp.int32)
    strip_pick = jax.random.randint(key_strip, (N_FROW, N_FCOL), 0, F // R, dtype=jnp.int32)
    facet_col = jax.random.randint(key_cols, (N_FROW, N_FCOL), 0, N // F, dtype=jnp.int32)
    row_first = facet_row * F + strip_pick * R
    col_first = facet_col * F
    row_first = row_first.at[0, 0].set(N - R)
    col_first = col_first.at[0, 0].set(0)
    return jnp.stack([row_first, col_first], -1).astype(jnp.int32)


def place_ends(array, rng, smallest, top_value):
    place = [jax.random.randint(jax.random.fold_in(rng, axis), (), 0, length) for axis, length in enumerate(array.shape)]
    longest = array.shape.index(max(array.shape))
    beside = place[:longest] + [(place[longest] + 1) % array.shape[longest]] + place[longest + 1:]
    return array.at[tuple(place)].set(smallest).at[tuple(beside)].set(top_value)


def level_of(stream_key, shape, shards, least, largest):
    loudness, own = 1.0, jax.random.fold_in(stream_key, 6)
    for dim, parts in shards:
        heights = jnp.exp(jax.random.uniform(jax.random.fold_in(own, dim), (parts,), jnp.float32, least / len(shards), largest / len(shards)))
        loudness = loudness * jnp.repeat(heights, shape[dim] // parts).reshape([-1 if axis == dim else 1 for axis in range(len(shape))])
    return loudness


def noise(stream_key, shape, width, bound, pieces=(), kind=jnp.bfloat16):
    factor_of = level_of(stream_key, shape, pieces, -0.22, 0.18) if pieces else 1.0
    values = jax.random.normal(stream_key, shape, jnp.float32) * width * factor_of
    return jnp.minimum(jnp.maximum(values, -bound), bound).astype(kind)


def setup_inputs(seed: int = 0) -> dict:
    key_of = jax.random.split(jax.random.key(seed), 9)
    return {
        "strips": noise(key_of[0], (2, N_FROW * R, N_FCOL * F), 1.0, 6.0, ((1, 4), (2, 8))),
        "row_window": jnp.clip(jnp.exp(jax.random.uniform(key_of[1], (F,), jnp.float32, math.log(0.5), math.log(2.0))), 0.5, 2.0),
        "col_window": jnp.clip(jnp.exp(jax.random.uniform(key_of[2], (F,), jnp.float32, math.log(0.5), math.log(2.0))), 0.5, 2.0),
        "sub_rows": place_ends(jax.random.randint(key_of[3], (SG_R,), 0, N), jax.random.fold_in(key_of[3], 1), 0, N - 1).astype(jnp.int32),
        "sub_cols": place_ends(jax.random.randint(key_of[4], (SG_C,), 0, N), jax.random.fold_in(key_of[4], 1), 0, N - 1).astype(jnp.int32),
        "facet_offsets": draw_facet_offsets(jax.random.fold_in(key_of[8], 71), 0),
        "owner_map": jax.random.permutation(key_of[6], PIECES).astype(jnp.int32),
        "screens": jnp.clip(jax.random.uniform(key_of[7], (2, PIECES, S, S // 2), jnp.float32, -1.5, 1.5) * level_of(key_of[7], (2, PIECES, S, S // 2), ((1, 8), (2, 4)), -0.4, 0.0), -1.5, 1.5),
    }


def mod_product(first_factor, second_factor, modulus):
    upper_part = first_factor // 256
    lower_part = first_factor % 256
    return (upper_part * second_factor % modulus * 256 + lower_part * second_factor) % modulus

def column_table(first_col, offset, col_window):
    lane_ids = jnp.arange(M, dtype=jnp.int32)
    positions = first_col + jnp.arange(F, dtype=jnp.int32)
    frequency = (offset + lane_ids) % N
    phases = mod_product(positions[None, :], frequency[:, None], N).astype(jnp.float32) * (2.0 * math.pi / N)
    col_real = (col_window[None, :] * jnp.cos(phases)).astype(jnp.bfloat16)
    col_imag = (-col_window[None, :] * jnp.sin(phases)).astype(jnp.bfloat16)
    return (col_real, col_imag)

def row_table(first_row, offset, row_window):
    lane_ids = jnp.arange(M, dtype=jnp.int32)
    positions = first_row + jnp.arange(R, dtype=jnp.int32)
    frequency = (offset + lane_ids) % N
    window = lax.dynamic_slice_in_dim(row_window, (first_row % F).astype(jnp.int32), R)
    phases = mod_product(positions[None, :], frequency[:, None], N).astype(jnp.float32) * (2.0 * math.pi / N)
    row_real = (window[None, :] * jnp.cos(phases)).astype(jnp.bfloat16)
    row_imag = (-window[None, :] * jnp.sin(phases)).astype(jnp.bfloat16)
    return (row_real, row_imag)

def expansion_table(band_shift, first_index, length):
    lane_ids = jnp.arange(M, dtype=jnp.int32)
    pixel_ids = first_index + jnp.arange(length, dtype=jnp.int32)
    shifted = lane_ids[None, :] + jnp.expand_dims(band_shift, (-1, -2))
    phases = (pixel_ids[:, None] * shifted % S).astype(jnp.float32) * (2.0 * math.pi / S)
    return (jnp.cos(phases).astype(jnp.bfloat16), jnp.sin(phases).astype(jnp.bfloat16))

def contribution(strip_data, first_row, first_col, row_window, col_window, sub_rows, sub_cols):
    strip_real = strip_data[0]
    strip_imag = strip_data[1]
    partials = []
    for col_pick in range(SG_C):
        col_real, col_imag = column_table(first_col, sub_cols[col_pick], col_window)
        partial_real = jnp.dot(strip_real, col_real.T, preferred_element_type=jnp.float32) - jnp.dot(strip_imag, col_imag.T, preferred_element_type=jnp.float32)
        partial_imag = jnp.dot(strip_real, col_imag.T, preferred_element_type=jnp.float32) + jnp.dot(strip_imag, col_real.T, preferred_element_type=jnp.float32)
        partials.append((partial_real.astype(jnp.bfloat16), partial_imag.astype(jnp.bfloat16)))
    factor = 1.0 / math.sqrt(R * F)
    blocks = []
    for row_pick in range(SG_R):
        row_real, row_imag = row_table(first_row, sub_rows[row_pick], row_window)
        for partial_real, partial_imag in partials:
            contrib_real = (jnp.dot(row_real, partial_real, preferred_element_type=jnp.float32) - jnp.dot(row_imag, partial_imag, preferred_element_type=jnp.float32)) * factor
            contrib_imag = (jnp.dot(row_real, partial_imag, preferred_element_type=jnp.float32) + jnp.dot(row_imag, partial_real, preferred_element_type=jnp.float32)) * factor
            blocks.append(jnp.stack([contrib_real, contrib_imag]).astype(jnp.bfloat16))
    return jnp.stack(blocks)

def reference(strips, row_window, col_window, sub_rows, sub_cols, facet_offsets, owner_map, screens):
    subgrid_total = SG_R * SG_C
    strip_total = N_FROW * N_FCOL
    factor = 1.0 / math.sqrt(M)

    def accumulate(subgrid_sum, strip_id):
        facet_row = strip_id // N_FCOL
        facet_col = strip_id % N_FCOL
        strip_data = lax.dynamic_slice(strips, (jnp.int32(0), (facet_row * R).astype(jnp.int32), (facet_col * F).astype(jnp.int32)), (2, R, F))
        first_row = facet_offsets[facet_row, facet_col, 0]
        first_col = facet_offsets[facet_row, facet_col, 1]
        contrib = contribution(strip_data, first_row, first_col, row_window, col_window, sub_rows, sub_cols).astype(jnp.float32)
        table_real, table_imag = expansion_table(first_col * S // N % S, 0, S)
        table_real = table_real.astype(jnp.float32)
        table_imag = table_imag.astype(jnp.float32)
        expanded_real = (jnp.einsum('gkl,jl->gkj', contrib[:, 0], table_real) - jnp.einsum('gkl,jl->gkj', contrib[:, 1], table_imag)) * factor
        expanded_imag = (jnp.einsum('gkl,jl->gkj', contrib[:, 0], table_imag) + jnp.einsum('gkl,jl->gkj', contrib[:, 1], table_real)) * factor
        expanded = lax.optimization_barrier(jnp.stack([expanded_real, expanded_imag], 1).astype(jnp.bfloat16)).astype(jnp.float32)
        padded = jnp.pad(expanded, ((0, 0), (0, 0), (0, S - M), (0, 0)))
        placed = jnp.roll(padded, first_row * S // N % S, axis=2)
        return (subgrid_sum + placed, None)
    initial = jnp.zeros((subgrid_total, 2, S, S), jnp.float32)
    subgrid_sum, unused = lax.scan(accumulate, initial, jnp.arange(strip_total, dtype=jnp.int32))
    subgrid_sum = subgrid_sum * (2.0 / math.sqrt(strip_total))
    halves = subgrid_sum.reshape(subgrid_total, 2, S, 2, S // 2).transpose(0, 3, 1, 2, 4).reshape(2 * subgrid_total, 2, S, S // 2)
    chosen = jnp.take(halves, owner_map, axis=0)
    grid_real = chosen[:, 0]
    grid_imag = chosen[:, 1]
    screen_real = screens[0]
    screen_imag = screens[1]
    return jnp.stack([screen_real * grid_real - screen_imag * grid_imag, screen_real * grid_imag + screen_imag * grid_real], 0)
```

```python
import math

import jax
import jax.numpy as jnp
import ml_dtypes
import numpy as np
from jax import lax
from jax.sharding import PartitionSpec as P

N = 65536
F = 4096
R = 64
M = 128
S = 512
SG_R = 4
SG_C = 4
PIECES = 32
CHUNK = 32


def mod_product(first_factor, second_factor):
    upper_part = first_factor // 256
    lower_part = first_factor % 256
    return (((upper_part * second_factor) & (N - 1)) * 256 + lower_part * second_factor) & (N - 1)


def turn(phase, period):
    angle = phase.astype(jnp.float32) * (2.0 * math.pi / period)
    return jnp.cos(angle), jnp.sin(angle)


def dft_constant():
    phase = (np.arange(F)[:, None] * np.arange(M)[None, :] % N) * (2.0 * math.pi / N)
    return np.concatenate([np.cos(phase), -np.sin(phase)], 1).astype(ml_dtypes.bfloat16)


def expansion_constant():
    phase = (np.arange(M)[:, None] * np.arange(S // 2)[None, :] % S) * (2.0 * math.pi / S)
    return np.cos(phase).astype(np.float32), np.sin(phase).astype(np.float32)


def partials(strips, first_col, col_window, sub_cols):
    positions = first_col + jnp.arange(F, dtype=jnp.int32)
    cos, sin = turn(mod_product(positions[None, :], sub_cols[:, None]), N)
    real = (col_window[None, :] * cos)[:, None]
    imag = (-col_window[None, :] * sin)[:, None]
    strip_real = strips[0].astype(jnp.float32)[None]
    strip_imag = strips[1].astype(jnp.float32)[None]
    turned = jnp.stack(
        [strip_real * real - strip_imag * imag, strip_real * imag + strip_imag * real], 1
    ).astype(jnp.bfloat16)
    product = jnp.dot(
        turned.reshape(SG_C * 2 * R, F), jnp.asarray(dft_constant()), preferred_element_type=jnp.float32
    ).reshape(SG_C, 2, R, 2, M)
    part_real = product[:, 0, :, 0] - product[:, 1, :, 1]
    part_imag = product[:, 0, :, 1] + product[:, 1, :, 0]
    band = first_col // (N // S)
    cos, sin = turn((band * jnp.arange(M, dtype=jnp.int32)) & (S - 1), S)
    return jnp.concatenate(
        [part_real * cos + part_imag * sin, part_imag * cos - part_real * sin], -1
    ).astype(jnp.bfloat16)


def expansion(band):
    base_real, base_imag = expansion_constant()
    cos, sin = turn((band[:, None] * jnp.arange(S // 2, dtype=jnp.int32)) & (S - 1), S)
    real = base_real[None] * cos[:, None] - base_imag[None] * sin[:, None]
    imag = base_real[None] * sin[:, None] + base_imag[None] * cos[:, None]
    return jnp.concatenate(
        [jnp.concatenate([real, imag], -1), jnp.concatenate([-imag, real], -1)], 1
    ).astype(jnp.bfloat16)


def placed_rows(first_row, row_start, rows, row_window, slot_rows):
    inner = jnp.arange(R, dtype=jnp.int32)
    window = jax.vmap(lambda start: lax.dynamic_slice_in_dim(row_window, start, R))(first_row % F)
    position = (first_row[:, None] + inner[None]).reshape(1, -1)
    shift = (row_start - first_row // (N // S)) & (S - 1)
    shift = jnp.where(shift < M, shift, shift - S)
    row_ids = jnp.arange(rows, dtype=jnp.int32)[:, None]
    row_index = row_ids + jnp.repeat(shift, R)[None]
    scale = jnp.where((row_index >= 0) & (row_index < M), window.reshape(1, -1), 0.0)
    base_cos, base_sin = turn((row_ids * position) & (N - 1), N)
    base_cos = base_cos * scale
    base_sin = base_sin * scale
    frequency = (slot_rows[:, None] + jnp.repeat(shift, R)[None]) & (N - 1)
    cos, sin = turn(mod_product(position, frequency), N)
    real = base_cos[None] * cos[:, None] - base_sin[None] * sin[:, None]
    imag = -(base_cos[None] * sin[:, None] + base_sin[None] * cos[:, None])
    return jnp.stack([real, imag], 1).astype(jnp.bfloat16)


def shards(strips, row_window, col_window, sub_rows, sub_cols, facet_offsets, owner_map, screens):
    row_index = lax.axis_index("frow")
    col_index = lax.axis_index("fcol")
    col_count = lax.axis_size("fcol")
    row_devices = lax.axis_size("frow")
    slot_count = PIECES // col_count
    rows = S // row_devices
    sources = row_devices * col_count
    own = partials(strips, facet_offsets[row_index, col_index, 1], col_window, sub_cols)
    slots = lax.dynamic_slice_in_dim(owner_map, col_index * slot_count, slot_count)
    if slot_count < SG_C:
        outgoing = jnp.take(own, owner_map // 2 % SG_C, axis=0)
        picked = lax.all_to_all(outgoing, "fcol", split_axis=0, concat_axis=0, tiled=True)
        picked = picked.reshape(col_count, slot_count, R, 2 * M)
        picked = lax.all_gather(picked, "frow", tiled=True)
    else:
        picked = lax.all_gather(own, ("frow", "fcol"))
        picked = jnp.take(picked, slots // 2 % SG_C, axis=1)
    lanes = jnp.arange(2 * M, dtype=jnp.int32)
    signs = (1 - 2 * ((lanes[None] * (slots % 2)[:, None]) & 1)).astype(jnp.bfloat16)
    picked = picked * signs[None, :, None, :]
    first = facet_offsets.reshape(sources, 2)
    slot_rows = sub_rows[slots // (2 * SG_C)]

    def gather_part(first, picked):
        count = first.shape[0]
        row_part = placed_rows(first[:, 0], row_index * rows, rows, row_window, slot_rows)
        table = expansion(first[:, 1] // (N // S))
        spread = jnp.einsum("nsxk,nkv->snxv", picked, table, preferred_element_type=jnp.float32)
        spread = spread.astype(jnp.bfloat16).reshape(slot_count, count * R, S)
        return jnp.einsum(
            "spkc,scv->spkv", row_part, spread, preferred_element_type=jnp.float32
        )

    chunk = min(CHUNK, sources)
    if sources == chunk:
        total = gather_part(first, picked)
    else:
        steps = sources // chunk
        total, unused = lax.scan(
            lambda carry, item: (carry + gather_part(*item), None),
            jnp.zeros((slot_count, 2, rows, S), jnp.float32),
            (first.reshape(steps, chunk, 2), picked.reshape(steps, chunk, slot_count, R, 2 * M)),
        )
    half = S // 2
    weight = 2.0 / math.sqrt(sources) / math.sqrt(M) / math.sqrt(R * F)
    grid_real = (total[:, 0, :, :half] - total[:, 1, :, half:]) * weight
    grid_imag = (total[:, 0, :, half:] + total[:, 1, :, :half]) * weight
    return jnp.stack(
        [
            screens[0] * grid_real - screens[1] * grid_imag,
            screens[0] * grid_imag + screens[1] * grid_real,
        ],
        0,
    )


def solution(mesh):
    return jax.shard_map(
        shards,
        mesh=mesh,
        in_specs=(
            P(None, "frow", "fcol"),
            P(),
            P(),
            P(),
            P(),
            P(),
            P(),
            P(None, "fcol", "frow", None),
        ),
        out_specs=P(None, "fcol", "frow", None),
        check_vma=False,
    )
```

```python
import math

import jax
import jax.numpy as jnp
import ml_dtypes
import numpy as np
from jax import lax
from jax.experimental import pallas as pl
from jax.experimental.pallas import tpu as pltpu
from jax.sharding import PartitionSpec as P

N = 65536
F = 4096
R = 64
M = 128
S = 512
SG_R = 4
SG_C = 4
PIECES = 32
CHUNK = 32


def mod_product(first_factor, second_factor):
    upper_part = first_factor // 256
    lower_part = first_factor % 256
    return (((upper_part * second_factor) & (N - 1)) * 256 + lower_part * second_factor) & (N - 1)


def turn(phase, period):
    angle = phase.astype(jnp.float32) * (2.0 * math.pi / period)
    return jnp.cos(angle), jnp.sin(angle)


def dft_constant():
    phase = (np.arange(F)[:, None] * np.arange(M)[None, :] % N) * (2.0 * math.pi / N)
    return np.concatenate([np.cos(phase), -np.sin(phase)], 1).astype(ml_dtypes.bfloat16)


def expansion_constant():
    phase = (np.arange(M)[:, None] * np.arange(S // 2)[None, :] % S) * (2.0 * math.pi / S)
    return np.cos(phase).astype(np.float32), np.sin(phase).astype(np.float32)


def partials(strips, first_col, col_window, sub_cols):
    positions = first_col + jnp.arange(F, dtype=jnp.int32)
    cos, sin = turn(mod_product(positions[None, :], sub_cols[:, None]), N)
    real = (col_window[None, :] * cos)[:, None]
    imag = (-col_window[None, :] * sin)[:, None]
    strip_real = strips[0].astype(jnp.float32)[None]
    strip_imag = strips[1].astype(jnp.float32)[None]
    turned = jnp.stack(
        [strip_real * real - strip_imag * imag, strip_real * imag + strip_imag * real], 1
    ).astype(jnp.bfloat16)
    product = jnp.dot(
        turned.reshape(SG_C * 2 * R, F), jnp.asarray(dft_constant()), preferred_element_type=jnp.float32
    ).reshape(SG_C, 2, R, 2, M)
    part_real = product[:, 0, :, 0] - product[:, 1, :, 1]
    part_imag = product[:, 0, :, 1] + product[:, 1, :, 0]
    band = first_col // (N // S)
    cos, sin = turn((band * jnp.arange(M, dtype=jnp.int32)) & (S - 1), S)
    return jnp.concatenate(
        [part_real * cos + part_imag * sin, part_imag * cos - part_real * sin], -1
    ).astype(jnp.bfloat16)


def expansion(band):
    base_real, base_imag = expansion_constant()
    cos, sin = turn((band[:, None] * jnp.arange(S // 2, dtype=jnp.int32)) & (S - 1), S)
    real = base_real[None] * cos[:, None] - base_imag[None] * sin[:, None]
    imag = base_real[None] * sin[:, None] + base_imag[None] * cos[:, None]
    return jnp.concatenate(
        [jnp.concatenate([real, imag], -1), jnp.concatenate([-imag, real], -1)], 1
    ).astype(jnp.bfloat16)


def strip_windows(first_row, row_window):
    picks = (first_row % F) // R
    onehot = picks[:, None] == jnp.arange(F // R, dtype=jnp.int32)[None]
    return jnp.sum(jnp.where(onehot[:, :, None], row_window.reshape(1, F // R, R), 0.0), 1)


def placed_rows(first_row, row_start, rows, row_window, slot_rows):
    inner = jnp.arange(R, dtype=jnp.int32)
    window = strip_windows(first_row, row_window)
    position = (first_row[:, None] + inner[None]).reshape(1, -1)
    shift = (row_start - first_row // (N // S)) & (S - 1)
    shift = jnp.where(shift < M, shift, shift - S)
    row_ids = jnp.arange(rows, dtype=jnp.int32)[:, None]
    row_index = row_ids + jnp.repeat(shift, R)[None]
    scale = jnp.where((row_index >= 0) & (row_index < M), window.reshape(1, -1), 0.0)
    base_cos, base_sin = turn((row_ids * position) & (N - 1), N)
    base_cos = base_cos * scale
    base_sin = base_sin * scale
    frequency = (slot_rows[:, None] + jnp.repeat(shift, R)[None]) & (N - 1)
    cos, sin = turn(mod_product(position, frequency), N)
    real = base_cos[None] * cos[:, None] - base_sin[None] * sin[:, None]
    imag = -(base_cos[None] * sin[:, None] + base_sin[None] * cos[:, None])
    return jnp.stack([real, imag], 1).astype(jnp.bfloat16)


def flip(index, bits, size):
    result = index
    step = 1
    while step < size:
        if bits & step:
            result = result + step - 2 * step * ((index // step) % 2)
        step *= 2
    return result


def gather_kernel(chips, own_ref, out_ref, send_sem, recv_sem, own_sem):
    row = lax.axis_index("frow")
    col = lax.axis_index("fcol")
    core = col % 2
    chip = col // 2
    sent = []

    def device(row_bits, chip_bits, core_bits):
        return (
            flip(row, row_bits, 4),
            2 * flip(chip, chip_bits, chips) + flip(core, core_bits, 2),
        )

    def place(row_bits, chip_bits, core_bits):
        there = device(row_bits, chip_bits, core_bits)
        return there[0] * (2 * chips) + there[1]

    def send(item, target):
        source = own_ref if item == (0, 0, 0) else out_ref.at[place(*item)]
        copy = pltpu.make_async_remote_copy(
            src_ref=source,
            dst_ref=out_ref.at[place(*item)],
            send_sem=send_sem.at[len(sent)],
            recv_sem=recv_sem.at[place(*item)],
            device_id=device(*target),
            device_id_type=pl.DeviceIdType.MESH,
        )
        copy.start()
        sent.append(copy)

    def arrived(item):
        there = out_ref.at[place(*item)]
        pltpu.make_async_copy(there, there, recv_sem.at[place(*item)]).wait()

    across, along, partner = (1, 0, 0), (2, 0, 0), (0, 0, 1)
    peers = [across, along, partner] + [(0, bits, 0) for bits in range(1, chips)]
    barrier = pltpu.get_barrier_semaphore()
    for peer in peers:
        pl.semaphore_signal(
            barrier, inc=1, device_id=device(*peer), device_id_type=pl.DeviceIdType.MESH
        )
    pl.semaphore_wait(barrier, len(peers))
    mine = (0, 0, 0)
    for peer in peers[3:] + [across, along, partner]:
        send(mine, peer)
    keep = pltpu.make_async_copy(own_ref, out_ref.at[place(*mine)], own_sem)
    keep.start()
    for bits in range(chips):
        if bits:
            item = (0, bits, 0)
            arrived(item)
            for peer in (across, along, partner):
                send(item, peer)
        for first, other in ((1, along), (2, across)):
            item = (first, bits, 0)
            arrived(item)
            if (bits % 2 == 0) == (first == 1):
                send(item, other)
            send(item, partner)
    for bits in range(chips):
        item = (3, bits, 0)
        arrived(item)
        send(item, partner)
    for row_bits in range(4):
        for bits in range(chips):
            arrived((row_bits, bits, 1))
    for copy in sent:
        copy.wait_send()
    keep.wait()


def gather_all(own, sources, chips):
    sends = sources - 1
    return pl.pallas_call(
        lambda *refs: gather_kernel(chips, *refs),
        out_shape=jax.ShapeDtypeStruct((sources,) + own.shape, own.dtype),
        in_specs=[pl.BlockSpec(memory_space=pltpu.VMEM)],
        out_specs=pl.BlockSpec(memory_space=pl.ANY),
        scratch_shapes=[
            pltpu.SemaphoreType.DMA((sends,)),
            pltpu.SemaphoreType.DMA((sources,)),
            pltpu.SemaphoreType.DMA,
        ],
        compiler_params=pltpu.CompilerParams(collective_id=0, has_side_effects=True),
        name="gather_all",
    )(own)


def shards(strips, row_window, col_window, sub_rows, sub_cols, facet_offsets, owner_map, screens):
    row_index = lax.axis_index("frow")
    col_index = lax.axis_index("fcol")
    col_count = lax.axis_size("fcol")
    row_devices = lax.axis_size("frow")
    slot_count = PIECES // col_count
    rows = S // row_devices
    sources = row_devices * col_count
    own = partials(strips, facet_offsets[row_index, col_index, 1], col_window, sub_cols)
    slots = lax.dynamic_slice_in_dim(owner_map, col_index * slot_count, slot_count)
    if slot_count < SG_C:
        outgoing = jnp.take(own, owner_map // 2 % SG_C, axis=0)
        picked = lax.all_to_all(outgoing, "fcol", split_axis=0, concat_axis=0, tiled=True)
        picked = picked.reshape(col_count, slot_count, R, 2 * M)
        picked = lax.all_gather(picked, "frow", tiled=True)
    else:
        if row_devices == 4 and col_count == 8:
            picked = gather_all(own.reshape(SG_C * R, 2 * M), sources, col_count // 2)
            picked = picked.reshape(sources, SG_C, R, 2 * M)
        else:
            picked = lax.all_gather(own, ("frow", "fcol"))
        picked = jnp.take(picked, slots // 2 % SG_C, axis=1)
    lanes = jnp.arange(2 * M, dtype=jnp.int32)
    signs = (1 - 2 * ((lanes[None] * (slots % 2)[:, None]) & 1)).astype(jnp.bfloat16)
    picked = picked * signs[None, :, None, :]
    first = facet_offsets.reshape(sources, 2)
    slot_rows = sub_rows[slots // (2 * SG_C)]

    def gather_part(first, picked):
        count = first.shape[0]
        row_part = placed_rows(first[:, 0], row_index * rows, rows, row_window, slot_rows)
        table = expansion(first[:, 1] // (N // S))
        spread = jnp.einsum("nsxk,nkv->snxv", picked, table, preferred_element_type=jnp.float32)
        spread = spread.astype(jnp.bfloat16).reshape(slot_count, count * R, S)
        return jnp.einsum(
            "spkc,scv->spkv", row_part, spread, preferred_element_type=jnp.float32
        )

    chunk = min(CHUNK, sources)
    if sources == chunk:
        total = gather_part(first, picked)
    else:
        steps = sources // chunk
        total, unused = lax.scan(
            lambda carry, item: (carry + gather_part(*item), None),
            jnp.zeros((slot_count, 2, rows, S), jnp.float32),
            (first.reshape(steps, chunk, 2), picked.reshape(steps, chunk, slot_count, R, 2 * M)),
        )
    half = S // 2
    weight = 2.0 / math.sqrt(sources) / math.sqrt(M) / math.sqrt(R * F)
    grid_real = (total[:, 0, :, :half] - total[:, 1, :, half:]) * weight
    grid_imag = (total[:, 0, :, half:] + total[:, 1, :, :half]) * weight
    return jnp.stack(
        [
            screens[0] * grid_real - screens[1] * grid_imag,
            screens[0] * grid_imag + screens[1] * grid_real,
        ],
        0,
    )


def solution(mesh):
    return jax.shard_map(
        shards,
        mesh=mesh,
        in_specs=(
            P(None, "frow", "fcol"),
            P(),
            P(),
            P(),
            P(),
            P(),
            P(),
            P(None, "fcol", "frow", None),
        ),
        out_specs=P(None, "fcol", "frow", None),
        check_vma=False,
    )
```
